32 devices in a mesh: row: 4 (over x, core), col: 8 (over z, y).
Axes of the slice: x: 2, y: 2, z: 4, core: 2. Of those that a mesh axis runs over, the one named last changes fastest.
Arguments:
- adj_trailing: bfloat16 [4096, 8192], P('row', 'col'), may hold values from -6 to 6
- panel_rows0: bfloat16 [4096, 512], P('row'), may hold values from -0.09375 to 0.09375
- panel_rows1: bfloat16 [4096, 512], P('row'), may hold values from -0.09375 to 0.09375
- panel_cols0: bfloat16 [8192, 512], P('col'), may hold values from -0.0625 to 0.0625
- panel_cols1: bfloat16 [8192, 512], P('col'), may hold values from -0.0625 to 0.0625
- inv_diag0: float32 [512, 512], replicated, as said below
- inv_diag1: float32 [512, 512], replicated, as said below
- cross_block: float32 [512, 512], replicated, may hold values from -0.25 to 0.25
- panel_adj0: bfloat16 [4096, 512], P(('row', 'col')), may hold values from -6 to 6
- panel_adj1: bfloat16 [4096, 512], P(('row', 'col')), may hold values from -6 to 6
Outputs:
- row_adj1: float32 [4096, 512], P(('row', 'col'))
- row_adj0: float32 [4096, 512], P(('row', 'col'))
- col_adj1: float32 [8192, 512], P('col')
- col_adj0: float32 [8192, 512], P('col')
- diag_adj1: float32 [512, 512], replicated
- diag_adj0: float32 [512, 512], replicated
The draws below stay inside these ranges and needn't reach their ends.
Inputs may be any that keep to these rules, and one draw needn't show every extreme that they name: `inv_diag0`: lower triangular, with diagonal entries of 1 to 2. `inv_diag1`: lower triangular, with diagonal entries of 1 to 2.
All inputs are finite; a program needn't handle non-finite values.
Results may differ from the reference program's by a relative error of at most 0.0003.
Values sent between devices are 32-bit elements; how exact they have to be, the bound alone decides.
No kernel may reach another device: no remote copies, remote signals or barrier semaphores. Data moves between devices by JAX's collectives and lax.ppermute only.
A program may use at most 128 MiB of HBM per device.

```python
import math
import jax
import jax.numpy as jnp
from jax import lax

B = 512
ROWS = 4096
COLS = 8192


def inverse_factor(key):
    first, second = jax.random.split(key)
    index = jnp.arange(B)
    lower = index[:, None] > index[None, :]
    spread = jax.random.normal(first, (B, B), jnp.float32) * (0.6 / math.sqrt(B))
    diagonal = jax.random.uniform(second, (B,), jnp.float32, 1.0, 2.0)
    return jnp.where(lower, spread, 0.0) + jnp.diag(diagonal)


def draw_inv_diag0(key, part):
    return inverse_factor(jax.random.fold_in(key, 11))


def draw_inv_diag1(key, part):
    return inverse_factor(jax.random.fold_in(key, 23))


def levels(rng, dims, pieces, low, top_value):
    def one(axis_at, shards_of):
        draws = jax.random.uniform(jax.random.fold_in(jax.random.fold_in(rng, 6), axis_at), (shards_of,), jnp.float32, low / len(pieces), top_value / len(pieces))
        return jnp.repeat(jnp.exp(draws), dims[axis_at] // shards_of).reshape((-1,) + (1,) * (len(dims) - axis_at - 1))

    factor_of = one(*pieces[0])
    for cut in pieces[1:]:
        factor_of = factor_of * one(*cut)
    return factor_of


def scatter_about(rng, shape, width, bound, pieces=(), kind=jnp.bfloat16):
    factor_of = levels(rng, shape, pieces, -0.22, 0.18) if pieces else 1.0
    array = jax.random.normal(rng, shape, jnp.float32) * width * factor_of
    return jnp.minimum(jnp.maximum(array, -bound), bound).astype(kind)


def setup_inputs(seed: int = 0) -> dict:
    arg_keys = jax.random.split(jax.random.key(seed), 11)
    adj_trailing = scatter_about(arg_keys[0], (ROWS, COLS), 1.0, 6.0, ((0, 4), (1, 8)))
    panel_rows0 = scatter_about(arg_keys[1], (ROWS, B), ROWS ** -0.5, 0.09375, ((0, 4),))
    panel_rows1 = scatter_about(arg_keys[2], (ROWS, B), ROWS ** -0.5, 0.09375, ((0, 4),))
    panel_cols0 = scatter_about(arg_keys[3], (COLS, B), COLS ** -0.5, 0.0625, ((0, 8),))
    panel_cols1 = scatter_about(arg_keys[4], (COLS, B), COLS ** -0.5, 0.0625, ((0, 8),))
    inv_diag0 = draw_inv_diag0(jax.random.fold_in(arg_keys[10], 71), 0)
    inv_diag1 = draw_inv_diag1(jax.random.fold_in(arg_keys[10], 71), 0)
    cross_block = scatter_about(arg_keys[7], (B, B), B ** -0.5, 0.25, (), jnp.float32)
    panel_adj0 = scatter_about(arg_keys[8], (ROWS, B), 1.0, 6.0, ((0, 32),))
    panel_adj1 = scatter_about(arg_keys[9], (ROWS, B), 1.0, 6.0, ((0, 32),))
    return {"adj_trailing": adj_trailing, "panel_rows0": panel_rows0, "panel_rows1": panel_rows1, "panel_cols0": panel_cols0, "panel_cols1": panel_cols1, "inv_diag0": inv_diag0, "inv_diag1": inv_diag1, "cross_block": cross_block, "panel_adj0": panel_adj0, "panel_adj1": panel_adj1}


def reference(adj_trailing, panel_rows0, panel_rows1, panel_cols0, panel_cols1, inv_diag0, inv_diag1, cross_block, panel_adj0, panel_adj1):
    highest = lax.Precision.HIGHEST
    trail1 = jnp.dot(adj_trailing, panel_cols1, preferred_element_type=jnp.float32)
    trail0 = jnp.dot(adj_trailing, panel_cols0, preferred_element_type=jnp.float32)
    col_adj1 = -jnp.einsum("rc,rb->cb", adj_trailing, panel_rows1, preferred_element_type=jnp.float32)
    col_adj0 = -jnp.einsum("rc,rb->cb", adj_trailing, panel_rows0, preferred_element_type=jnp.float32)
    bar1 = panel_adj1.astype(jnp.float32) - trail1
    row_adj1 = jnp.dot(bar1, inv_diag1, precision=highest)
    bar0 = panel_adj0.astype(jnp.float32) - trail0 - jnp.dot(row_adj1, cross_block, precision=highest)
    row_adj0 = jnp.dot(bar0, inv_diag0, precision=highest)
    gram1 = jnp.dot(bar1.T, panel_rows1.astype(jnp.float32), precision=highest)
    gram0 = jnp.dot(bar0.T, panel_rows0.astype(jnp.float32), precision=highest)
    diag_adj1 = -jnp.tril(jnp.dot(inv_diag1.T, gram1, precision=highest))
    diag_adj0 = -jnp.tril(jnp.dot(inv_diag0.T, gram0, precision=highest))
    return (row_adj1, row_adj0, col_adj1, col_adj0, diag_adj1, diag_adj0)
```

```python
import functools

import jax
import jax.numpy as jnp
from jax import lax
from jax.experimental import pallas as pl
from jax.experimental.pallas import tpu as pltpu
from jax.sharding import PartitionSpec as P

F32 = jnp.float32
BF16 = jnp.bfloat16
LANES = 128

T_SHARES = ((1, 0, 4), (1, 4, 4), (0, 0, 4), (0, 4, 4))
C_SHARES = ((0, 2), (2, 4), (6, 2))


def mm(a, b):
    return jnp.dot(a, b, preferred_element_type=F32)


def mm_t(a, b):
    return lax.dot_general(a, b, (((0,), (0,)), ((), ())), preferred_element_type=F32)


def split2(x):
    hi = x.astype(BF16)
    return hi, (x - hi.astype(F32)).astype(BF16)


def split3(x):
    hi = x.astype(BF16)
    rest = x - hi.astype(F32)
    mid = rest.astype(BF16)
    return hi, mid, (rest - mid.astype(F32)).astype(BF16)


def mm3(a, b):
    ah, al = split2(a)
    bh, bl = split2(b)
    return mm(ah, bh) + (mm(ah, bl) + mm(al, bh))


SMEM = pl.BlockSpec(memory_space=pltpu.SMEM)
VMEM = pl.BlockSpec(memory_space=pltpu.VMEM)
ANY = pl.BlockSpec(memory_space=pl.ANY)


def f32(*shape):
    return jax.ShapeDtypeStruct(shape, F32)


def kernel(body, scalars, args, outs, flops=0, specs=None, out_specs=None, **more):
    specs = [VMEM] * len(args) if specs is None else specs
    out_specs = [VMEM] * len(outs) if out_specs is None else out_specs
    size = sum(a.size * a.dtype.itemsize for a in args)
    return pl.pallas_call(
        body,
        in_specs=[SMEM] + specs,
        out_specs=out_specs,
        out_shape=outs,
        cost_estimate=pl.CostEstimate(
            flops=int(flops), bytes_accessed=int(size), transcendentals=0
        ),
        compiler_params=pltpu.CompilerParams(vmem_limit_bytes=16 * 2**20),
        **more,
    )(scalars, *args)


CORE, PAIR, BIT = 0, 1, 2


def rows_of(ref, parity, blk):
    pairs = ref.shape[0] // (2 * blk)
    return jnp.concatenate(
        [ref[pl.ds(pl.multiple_of((2 * i + parity) * blk, blk), blk), :] for i in range(pairs)],
        axis=0,
    )


def trail_block(a, c_ref, start, o_ref):
    o_ref[...] = mm(a, c_ref[:, start : start + o_ref.shape[1]])


def column_block(at, r1_ref, r0_ref, o_ref):
    b = r1_ref.shape[1]
    o_ref[:, :b] = -mm_t(at, r1_ref[...])
    o_ref[:, b:] = -mm_t(at, r0_ref[...])


def window_cols(ref, start, side, half):
    return ref[:, pl.ds(pl.multiple_of(start + side * half, LANES), half)]


def trail_body(blk, plan, s, a_hbm, c1_hbm, c0_hbm, *refs):
    o_refs, (a_ref, c1_ref, c0_ref, sem) = refs[:-4], refs[-4:]
    pairs = a_ref.shape[1] // blk
    depth = c1_ref.shape[0] // 2
    loads = {0: [], 1: [], "c1": [], "c0": []}
    count = 0

    def load(key, src, dst):
        nonlocal count
        loads[key].append(pltpu.make_async_copy(src, dst, sem.at[count]))
        loads[key][-1].start()
        count += 1

    def load_rows(own):
        parity = s[BIT] if own else 1 - s[BIT]
        for i in range(pairs):
            at = pl.multiple_of((2 * i + parity) * blk, blk)
            load(own, a_hbm.at[pl.ds(at, blk)], a_ref.at[own, pl.ds(i * blk, blk)])

    def load_cols(key, src, dst):
        for i in range(2):
            at = pl.ds(i * depth, depth)
            load(key, src.at[at], dst.at[at])

    load_rows(0)
    load_cols("c1", c1_hbm, c1_ref)
    load_cols("c0", c0_hbm, c0_ref)
    load_rows(1)
    for (own, panel, start), o_ref in zip(plan, o_refs):
        for key in (own, "c1" if panel else "c0"):
            for c in loads[key]:
                c.wait()
            loads[key] = []
        trail_block(a_ref[own], c1_ref if panel else c0_ref, start, o_ref)


def column_body(sides, plan, s, a_ref, r1_ref, r0_ref, *o_refs):
    for own, o_ref in zip(sides, o_refs):
        side = s[CORE] if own else 1 - s[CORE]
        at = [window_cols(a_ref, start, side, half) for start, half in plan]
        column_block(jnp.concatenate(at, axis=1), r1_ref, r0_ref, o_ref)


def write_body(starts, s, *refs):
    n = len(starts)
    d1_ref, d0_ref, sem = refs[-3:]
    copies = []
    for k, start in enumerate(starts):
        for ref, side in ((refs[k], s[CORE]), (refs[n + k], 1 - s[CORE])):
            half, b = ref.shape[0], ref.shape[1] // 2
            at = pl.ds(pl.multiple_of(start + side * half, 8), half)
            for lanes, out in ((slice(0, b), d1_ref), (slice(b, 2 * b), d0_ref)):
                copies.append(
                    pltpu.make_async_copy(ref.at[:, lanes], out.at[at], sem.at[len(copies)])
                )
    for c in copies:
        c.start()
    for c in copies:
        c.wait()


def iotas(b):
    return (
        lax.broadcasted_iota(jnp.int32, (b, b), 0),
        lax.broadcasted_iota(jnp.int32, (b, b), 1),
    )


def diag_body(blk, n1, s, r1_ref, r0_ref, p1_ref, p0_ref, inv1_ref, inv0_ref, cross_ref, *refs):
    keep_ref, send_ref, g1, g10, g0, buf = refs[-6:]
    t_refs = refs[:-6]
    nt = len(t_refs) // 2
    b = inv1_ref.shape[0]
    h = b // 2
    for own in (0, 1):
        parity = s[BIT] if own else 1 - s[BIT]
        r1, r0 = rows_of(r1_ref, parity, blk), rows_of(r0_ref, parity, blk)
        n = r0.shape[0]
        place = lax.broadcasted_iota(jnp.int32, (n, 1), 0) // blk == s[PAIR]
        ts = t_refs[own * nt : (own + 1) * nt]
        for panel in (1, 0):
            mine = ts[:n1] if panel else ts[n1:]
            bar = -jnp.concatenate([t[...] for t in mine], axis=1)
            if own:
                p = (p1_ref if panel else p0_ref)[...].astype(F32)
                bar = bar + jnp.where(place, jnp.concatenate([p] * (n // blk), axis=0), 0.0)
            for side in (0, 1):
                at = slice(side * h, (side + 1) * h)
                parts = jnp.concatenate(split3(bar[:, at]), axis=1)
                top = b if side else h
                todo = [(g1, r1[:, :top]), (g10, r0)] if panel else [(g0, r0[:, :top])]
                for g, r in todo:
                    x = mm_t(r, parts)
                    x = x[:, :h] + (x[:, h : 2 * h] + x[:, 2 * h :])
                    k = r.shape[1]
                    if own:
                        x = x + g[:k, at]
                    g[:k, at] = x
    x10 = g10[...]
    left = mm3(x10, inv1_ref[:, :h])
    right = mm3(x10[:, h:], inv1_ref[h:, h:])
    x10 = jnp.concatenate([left, right], axis=1)
    g0[:h, :h] = g0[:h, :h] - mm3(x10[:h], cross_ref[:, :h])
    g0[:, h:] = g0[:, h:] - mm3(x10, cross_ref[:, h:])
    i, j = iotas(b)
    low = jnp.zeros((h, h), F32)

    def upper(g, inv_ref):
        left = mm3(g[:h, :], inv_ref[:, :h])
        right = mm3(g[:, h:], inv_ref[h:, h:])
        return jnp.concatenate([jnp.concatenate([left, low], axis=0), right], axis=1)

    l0 = upper(g0, inv0_ref)
    both = jnp.where(i <= j, upper(g1, inv1_ref), l0.T)
    diag = jnp.sum(jnp.where(i == j, l0, 0.0), axis=0, keepdims=True)
    k = b // LANES
    for p in range(k):
        buf[p * b : (p + 1) * b, :] = both[:, p * LANES : (p + 1) * LANES]
    buf[k * b :, :] = jnp.zeros((buf.shape[0] - k * b, LANES), F32)
    for p in range(k):
        buf[k * b + p : k * b + p + 1, :] = diag[:, p * LANES : (p + 1) * LANES]
    half = buf.shape[0] // 2
    core = s[CORE]
    keep_ref[...] = buf[pl.ds(pl.multiple_of(core * half, 8), half), :]
    send_ref[...] = buf[pl.ds(pl.multiple_of((1 - core) * half, 8), half), :]


def unpack_body(s, m_ref, t_ref, d1_ref, d0_ref, buf):
    half = m_ref.shape[0]
    core = s[CORE]
    buf[pl.ds(pl.multiple_of(core * half, 8), half), :] = m_ref[...]
    buf[pl.ds(pl.multiple_of((1 - core) * half, 8), half), :] = t_ref[...]
    b = d1_ref.shape[0]
    k = b // LANES
    m = jnp.concatenate([buf[p * b : (p + 1) * b, :] for p in range(k)], axis=1)
    diag = jnp.concatenate([buf[k * b + p : k * b + p + 1, :] for p in range(k)], axis=1)
    i, j = iotas(b)
    d1_ref[...] = -jnp.where(i <= j, m, 0.0).T
    d0_ref[...] = -jnp.where(i > j, m, jnp.where(i == j, diag, 0.0))


def gather_sums(refs):
    return jnp.concatenate([a[...] + b[...] for a, b in zip(refs[::2], refs[1::2])], axis=1)


def row1_body(s, p1_ref, p0_ref, inv1_ref, cross_ref, *refs):
    row1_ref, q_ref = refs[-2:]
    bar1 = p1_ref[...].astype(F32) - gather_sums(refs[:-2])
    row1 = mm3(bar1, inv1_ref[...])
    row1_ref[...] = row1
    q_ref[...] = p0_ref[...].astype(F32) - mm3(row1, cross_ref[...])


def row0_body(s, q_ref, inv0_ref, *refs):
    bar0 = q_ref[...] - gather_sums(refs[:-1])
    refs[-1][...] = mm3(bar0, inv0_ref[...])


def make_local(n_row, n_col):
    col_bits = n_col.bit_length() - 1
    row_bits = n_row.bit_length() - 1

    def swap(axis, a, bit):
        size = n_row if axis == "row" else n_col
        return lax.ppermute(a, axis, [(i, i ^ (1 << bit)) for i in range(size)])

    def body(adj, rows0, rows1, cols0, cols1, inv0, inv1, cross, p0, p1):
        rows, b = rows1.shape
        blk = p1.shape[0]
        window = adj.shape[1]
        me_row = lax.axis_index("row")
        me_col = lax.axis_index("col")
        bits = [(me_col >> k) % 2 for k in range(col_bits)]
        s = jnp.stack([me_row % 2, me_col // 2] + bits).astype(jnp.int32)
        sides = {("col", k): bit for k, bit in enumerate(bits)}
        sides |= {("row", k): (me_row >> k) % 2 for k in range(row_bits)}
        sides = {key: side.astype(jnp.uint32) for key, side in sides.items()}
        values = lax.optimization_barrier(
            (s, [(x, 1 - x, x == 0) for x in sides.values()])
        )
        s, sides = values[0], dict(zip(sides, values[1]))

        def pick(x, index):
            zero = jnp.uint32(0)
            shape = (x.shape[0], 1) + x.shape[2:]
            return lax.dynamic_slice(x, (zero, index, zero, zero), shape)

        def add(x, y):
            return x + y

        def add_split(x, y, key, split):
            x = add(x, y)
            n, w = x.shape
            x = x.reshape(n // (2 * split), 2, split, w)
            return tuple(
                pick(x, side).reshape(n // 2, w) for side in sides[key][:2]
            )

        def ordered(key, m, other):
            low = sides[key][2]
            return jnp.concatenate(
                [jnp.where(low, m, other), jnp.where(low, other, m)], axis=0
            )

        half_rows = rows // 2
        shares = [(p, st * b // 8, w * b // 8) for p, st, w in T_SHARES]
        windows = [(st * window // 8, w * window // 16) for st, w in C_SHARES]

        nt = len(shares)
        plan = [(own, p, st) for own in (0, 1) for p, st, _ in shares]
        out = kernel(
            functools.partial(trail_body, blk, plan),
            s,
            [adj, cols1, cols0],
            [f32(half_rows, w) for _, _, w in shares + shares],
            4 * rows * window * b,
            specs=[pl.BlockSpec(memory_space=pltpu.HBM)] * 3,
            scratch_shapes=[
                pltpu.VMEM((2, half_rows, window), adj.dtype),
                pltpu.VMEM((window, b), cols1.dtype),
                pltpu.VMEM((window, b), cols0.dtype),
                pltpu.SemaphoreType.DMA((n_col + 4,)),
            ],
        )
        t_other, t_own = list(out[:nt]), list(out[nt:])
        t_recv = [swap("col", t, 0) for t in t_other]

        def columns(sides, some):
            width = sum(w for _, w in some)
            return kernel(
                functools.partial(column_body, sides, some),
                s,
                [adj, rows1, rows0],
                [f32(width, 2 * b)] * len(sides),
                len(sides) * 4 * rows * width * b,
            )

        (c_other,) = columns((0,), windows[:1])
        c_recv = swap("row", c_other, 0)
        (c_own,) = columns((1,), windows[:1])
        sums = [add(c_own, c_recv)]
        c_other, c_own = columns((0, 1), windows[1:])
        c_recv = swap("row", c_other, 0)
        at = 0
        for _, w in windows[1:]:
            sums.append(c_own[at : at + w] + c_recv[at : at + w])
            at += w

        held, theirs = [], []
        for total in sums:
            for bit in range(1, row_bits):
                total = add(total, swap("row", total, bit))
            held.append(total)
            theirs.append(swap("row", total, 0))
        outs = []
        for ks in (range(len(sums) - 1), range(len(sums) - 1, len(sums))):
            args = [held[k] for k in ks] + [theirs[k] for k in ks]
            n = len(args)
            outs = list(
                kernel(
                    functools.partial(write_body, [windows[k][0] for k in ks]),
                    s,
                    args + outs,
                    [f32(window, b)] * 2,
                    specs=[VMEM] * n + [ANY] * len(outs),
                    out_specs=[ANY, ANY],
                    scratch_shapes=[pltpu.SemaphoreType.DMA((2 * n,))],
                    input_output_aliases={n + 1: 0, n + 2: 1} if outs else {},
                )
            )
        col_adj1, col_adj0 = outs

        parts = [key for key in (("row", 1), ("col", 1)) if key in sides]
        swaps = [("col", k) for k in range(2, col_bits)] + [("col", 0)]
        swaps += [("row", k) for k in range(2, row_bits)]
        pieces = 2 << len(parts)
        data = (b + 1) * (b // LANES)
        total_rows = -(-data // (8 * pieces)) * 8 * pieces
        n1 = sum(p for p, _, _ in shares)
        keep, send = kernel(
            functools.partial(diag_body, blk, n1),
            s,
            [rows1, rows0, p1, p0, inv1, inv0, cross] + t_other + t_own,
            [f32(total_rows // 2, LANES)] * 2,
            15 * rows * b * b + 15 * b**3,
            scratch_shapes=[pltpu.VMEM((b, b), F32)] * 3
            + [pltpu.VMEM((total_rows, LANES), F32)],
        )
        got = swap("row", send, 0)
        for key in parts:
            keep, send = add_split(keep, got, key, keep.shape[0] // 2)
            got = swap(key[0], send, key[1])
        m = add(keep, got)
        for key in swaps:
            m = add(m, swap(key[0], m, key[1]))
        for key in parts[::-1]:
            m = ordered(key, m, swap(key[0], m, key[1]))
        other = swap("row", m, 0)
        d1, d0 = kernel(
            unpack_body,
            s,
            [m, other],
            [f32(b, b)] * 2,
            scratch_shapes=[pltpu.VMEM((total_rows, LANES), F32)],
        )

        trail = {1: [], 0: []}
        for k, share in enumerate(shares):
            keep, got = t_own[k], t_recv[k]
            for bit in range(1, col_bits):
                keep, send = add_split(keep, got, ("col", bit), blk)
                got = swap("col", send, bit)
            trail[share[0]] += [keep, got]
        row1, q = kernel(
            row1_body, s, [p1, p0, inv1, cross] + trail[1], [f32(blk, b)] * 2, 12 * blk * b * b
        )
        (row0,) = kernel(row0_body, s, [q, inv0] + trail[0], [f32(blk, b)], 6 * blk * b * b)
        return row1, row0, col_adj1, col_adj0, d1, d0

    return body


def solution(mesh):
    return jax.shard_map(
        make_local(mesh.shape["row"], mesh.shape["col"]),
        mesh=mesh,
        in_specs=(
            P("row", "col"),
            P("row", None),
            P("row", None),
            P("col", None),
            P("col", None),
            P(),
            P(),
            P(),
            P(("row", "col"), None),
            P(("row", "col"), None),
        ),
        out_specs=(
            P(("row", "col"), None),
            P(("row", "col"), None),
            P("col", None),
            P("col", None),
            P(),
            P(),
        ),
        check_vma=False,
    )
```

```python
import functools

import jax
import jax.numpy as jnp
from jax import lax
from jax.experimental import pallas as pl
from jax.experimental.pallas import tpu as pltpu
from jax.sharding import PartitionSpec as P

F32 = jnp.float32
BF16 = jnp.bfloat16
LANES = 128

T_SHARES = ((1, 0, 6), (1, 6, 2), (0, 0, 4), (0, 4, 2), (0, 6, 2))
C_BLOCKS = ((0, 2, 1), (2, 6, 3))


def mm(a, b):
    return jnp.dot(a, b, preferred_element_type=F32)


def mm_t(a, b):
    return lax.dot_general(a, b, (((0,), (0,)), ((), ())), preferred_element_type=F32)


def split2(x):
    hi = x.astype(BF16)
    return hi, (x - hi.astype(F32)).astype(BF16)


def mm3(a, b):
    ah, al = split2(a)
    bh, bl = split2(b)
    return mm(ah, bh) + (mm(ah, bl) + mm(al, bh))


SMEM = pl.BlockSpec(memory_space=pltpu.SMEM)
VMEM = pl.BlockSpec(memory_space=pltpu.VMEM)
ANY = pl.BlockSpec(memory_space=pl.ANY)


def f32(*shape):
    return jax.ShapeDtypeStruct(shape, F32)


def kernel(body, scalars, args, outs, flops=0, specs=None, out_specs=None, **more):
    specs = [VMEM] * len(args) if specs is None else specs
    out_specs = [VMEM] * len(outs) if out_specs is None else out_specs
    size = sum(a.size * a.dtype.itemsize for a in args)
    return pl.pallas_call(
        body,
        in_specs=[SMEM] + specs,
        out_specs=out_specs,
        out_shape=outs,
        cost_estimate=pl.CostEstimate(
            flops=int(flops), bytes_accessed=int(size), transcendentals=0
        ),
        compiler_params=pltpu.CompilerParams(vmem_limit_bytes=16 * 2**20),
        **more,
    )(scalars, *args)


CORE, PAIR, BIT = 0, 1, 2


def rows_of(ref, parity, blk):
    pairs = ref.shape[0] // (2 * blk)
    return jnp.concatenate(
        [ref[pl.ds(pl.multiple_of((2 * i + parity) * blk, blk), blk), :] for i in range(pairs)],
        axis=0,
    )


def column_block(at, r1_ref, r0_ref, o_ref):
    b = r1_ref.shape[1]
    o_ref[:, :b] = -mm_t(at, r1_ref[...])
    o_ref[:, b:] = -mm_t(at, r0_ref[...])


def window_cols(ref, start, side, half):
    return ref[:, pl.ds(pl.multiple_of(start + side * half, LANES), half)]


def trail_body(blk, plan, s, a_hbm, c1_hbm, c0_hbm, *refs):
    o_refs, (a_ref, c1_ref, c0_ref, sem) = refs[:-4], refs[-4:]
    pairs = a_ref.shape[1] // blk
    depth = c1_ref.shape[0] // 2
    loads = {0: [], 1: [], "c1": [], "c0": []}
    count = 0

    def load(key, src, dst):
        nonlocal count
        loads[key].append(pltpu.make_async_copy(src, dst, sem.at[count]))
        loads[key][-1].start()
        count += 1

    def load_rows(own):
        parity = s[BIT] if own else 1 - s[BIT]
        for i in range(pairs):
            at = pl.multiple_of((2 * i + parity) * blk, blk)
            load(own, a_hbm.at[pl.ds(at, blk)], a_ref.at[own, pl.ds(i * blk, blk)])

    def load_cols(key, src, dst):
        for i in range(2):
            at = pl.ds(i * depth, depth)
            load(key, src.at[at], dst.at[at])

    load_rows(0)
    load_cols("c1", c1_hbm, c1_ref)
    load_cols("c0", c0_hbm, c0_ref)
    load_rows(1)
    for half in sorted({(own, 1 - panel) for own, panel, _ in plan}):
        own, panel = half[0], 1 - half[1]
        for key in (own, "c1" if panel else "c0"):
            for c in loads[key]:
                c.wait()
            loads[key] = []
        t = mm(a_ref[own], (c1_ref if panel else c0_ref)[...])
        for (*key, start), o_ref in zip(plan, o_refs):
            if key == [own, panel]:
                o_ref[...] = t[:, start : start + o_ref.shape[1]]


def column_body(sides, start, s, a_ref, r1_ref, r0_ref, *o_refs):
    for own, o_ref in zip(sides, o_refs):
        side = s[CORE] if own else 1 - s[CORE]
        column_block(window_cols(a_ref, start, side, o_ref.shape[0]), r1_ref, r0_ref, o_ref)


def write_body(places, s, *refs):
    n = len(places)
    d1_ref, d0_ref, sem = refs[-3:]
    copies = []
    for k, (start, stride) in enumerate(places):
        for ref, side in ((refs[k], s[CORE]), (refs[n + k], 1 - s[CORE])):
            half, b = ref.shape[0], ref.shape[1] // 2
            at = pl.ds(pl.multiple_of(start + side * stride, 8), half)
            for lanes, out in ((slice(0, b), d1_ref), (slice(b, 2 * b), d0_ref)):
                copies.append(
                    pltpu.make_async_copy(ref.at[:, lanes], out.at[at], sem.at[len(copies)])
                )
    for c in copies:
        c.start()
    for c in copies:
        c.wait()


def iotas(b):
    return (
        lax.broadcasted_iota(jnp.int32, (b, b), 0),
        lax.broadcasted_iota(jnp.int32, (b, b), 1),
    )


def diag_body(blk, n1, s, r1_ref, r0_ref, p1_ref, p0_ref, inv1_ref, inv0_ref, cross_ref, *refs):
    keep_ref, send_ref, g1, g10, g0, buf = refs[-6:]
    t_refs = refs[:-6]
    nt = len(t_refs) // 2
    b = inv1_ref.shape[0]
    h = b // 2
    for own in (0, 1):
        parity = s[BIT] if own else 1 - s[BIT]
        r1, r0 = rows_of(r1_ref, parity, blk), rows_of(r0_ref, parity, blk)
        n = r0.shape[0]
        place = lax.broadcasted_iota(jnp.int32, (n, 1), 0) // blk == s[PAIR]
        ts = t_refs[own * nt : (own + 1) * nt]
        for panel in (1, 0):
            mine = ts[:n1] if panel else ts[n1:]
            bar = -jnp.concatenate([t[...] for t in mine], axis=1)
            if own:
                p = (p1_ref if panel else p0_ref)[...].astype(F32)
                bar = bar + jnp.where(place, jnp.concatenate([p] * (n // blk), axis=0), 0.0)
            for side in (0, 1):
                at = slice(side * h, (side + 1) * h)
                parts = jnp.concatenate(split2(bar[:, at]), axis=1)
                top = b if side else h
                todo = [(g1, r1[:, :top]), (g10, r0)] if panel else [(g0, r0[:, :top])]
                for g, r in todo:
                    x = mm_t(r, parts)
                    x = x[:, :h] + x[:, h:]
                    k = r.shape[1]
                    if own:
                        x = x + g[:k, at]
                    g[:k, at] = x
    x10 = g10[...]
    left = mm3(x10, inv1_ref[:, :h])
    right = mm3(x10[:, h:], inv1_ref[h:, h:])
    x10 = jnp.concatenate([left, right], axis=1)
    g0[:h, :h] = g0[:h, :h] - mm3(x10[:h], cross_ref[:, :h])
    g0[:, h:] = g0[:, h:] - mm3(x10, cross_ref[:, h:])
    i, j = iotas(b)
    low = jnp.zeros((h, h), F32)

    def upper(g, inv_ref):
        left = mm3(g[:h, :], inv_ref[:, :h])
        right = mm3(g[:, h:], inv_ref[h:, h:])
        return jnp.concatenate([jnp.concatenate([left, low], axis=0), right], axis=1)

    l0 = upper(g0, inv0_ref)
    both = jnp.where(i <= j, upper(g1, inv1_ref), l0.T)
    diag = jnp.sum(jnp.where(i == j, l0, 0.0), axis=0, keepdims=True)
    k = b // LANES
    for p in range(k):
        buf[p * b : (p + 1) * b, :] = both[:, p * LANES : (p + 1) * LANES]
    buf[k * b :, :] = jnp.zeros((buf.shape[0] - k * b, LANES), F32)
    for p in range(k):
        buf[k * b + p : k * b + p + 1, :] = diag[:, p * LANES : (p + 1) * LANES]
    half = buf.shape[0] // 2
    core = s[CORE]
    keep_ref[...] = buf[pl.ds(pl.multiple_of(core * half, 8), half), :]
    send_ref[...] = buf[pl.ds(pl.multiple_of((1 - core) * half, 8), half), :]


def unpack_body(s, m_ref, t_ref, d1_ref, d0_ref, buf):
    half = m_ref.shape[0]
    core = s[CORE]
    buf[pl.ds(pl.multiple_of(core * half, 8), half), :] = m_ref[...]
    buf[pl.ds(pl.multiple_of((1 - core) * half, 8), half), :] = t_ref[...]
    b = d1_ref.shape[0]
    k = b // LANES
    m = jnp.concatenate([buf[p * b : (p + 1) * b, :] for p in range(k)], axis=1)
    diag = jnp.concatenate([buf[k * b + p : k * b + p + 1, :] for p in range(k)], axis=1)
    i, j = iotas(b)
    d1_ref[...] = -jnp.where(i <= j, m, 0.0).T
    d0_ref[...] = -jnp.where(i > j, m, jnp.where(i == j, diag, 0.0))


def gather_sums(refs):
    return jnp.concatenate([a[...] + b[...] for a, b in zip(refs[::2], refs[1::2])], axis=1)


def row1_body(s, p1_ref, p0_ref, inv1_ref, cross_ref, *refs):
    row1_ref, q_ref = refs[-2:]
    bar1 = p1_ref[...].astype(F32) - gather_sums(refs[:-2])
    row1 = mm3(bar1, inv1_ref[...])
    row1_ref[...] = row1
    q_ref[...] = p0_ref[...].astype(F32) - mm3(row1, cross_ref[...])


def row0_body(s, q_ref, inv0_ref, *refs):
    bar0 = q_ref[...] - gather_sums(refs[:-1])
    refs[-1][...] = mm3(bar0, inv0_ref[...])


def make_local(n_row, n_col):
    col_bits = n_col.bit_length() - 1
    row_bits = n_row.bit_length() - 1

    def swap(axis, a, bit):
        size = n_row if axis == "row" else n_col
        return lax.ppermute(a, axis, [(i, i ^ (1 << bit)) for i in range(size)])

    def body(adj, rows0, rows1, cols0, cols1, inv0, inv1, cross, p0, p1):
        rows, b = rows1.shape
        blk = p1.shape[0]
        window = adj.shape[1]
        me_row = lax.axis_index("row")
        me_col = lax.axis_index("col")
        bits = [(me_col >> k) % 2 for k in range(col_bits)]
        s = jnp.stack([me_row % 2, me_col // 2] + bits).astype(jnp.int32)
        sides = {("col", k): bit for k, bit in enumerate(bits)}
        sides |= {("row", k): (me_row >> k) % 2 for k in range(row_bits)}
        sides = {key: side.astype(jnp.uint32) for key, side in sides.items()}
        values = lax.optimization_barrier(
            (s, [(x, 1 - x, x == 0) for x in sides.values()])
        )
        s, sides = values[0], dict(zip(sides, values[1]))

        def pick(x, index):
            zero = jnp.uint32(0)
            shape = (x.shape[0], 1) + x.shape[2:]
            return lax.dynamic_slice(x, (zero, index, zero, zero), shape)

        def add(x, y):
            return x + y

        def add_split(x, y, key, split):
            x = add(x, y)
            n, w = x.shape
            x = x.reshape(n // (2 * split), 2, split, w)
            return tuple(
                pick(x, side).reshape(n // 2, w) for side in sides[key][:2]
            )

        def ordered(key, m, other):
            low = sides[key][2]
            return jnp.concatenate(
                [jnp.where(low, m, other), jnp.where(low, other, m)], axis=0
            )

        half_rows = rows // 2
        shares = [(p, st * b // 8, w * b // 8) for p, st, w in T_SHARES]
        blocks = [(st * window // 8, w * window // 16, cuts) for st, w, cuts in C_BLOCKS]

        nt = len(shares)
        plan = [(own, p, st) for own in (0, 1) for p, st, _ in shares]
        out = kernel(
            functools.partial(trail_body, blk, plan),
            s,
            [pltpu.with_memory_space_constraint(x, pltpu.HBM) for x in (adj, cols1, cols0)],
            [f32(half_rows, w) for _, _, w in shares + shares],
            4 * rows * window * b,
            specs=[pl.BlockSpec(memory_space=pltpu.HBM)] * 3,
            scratch_shapes=[
                pltpu.VMEM((2, half_rows, window), adj.dtype),
                pltpu.VMEM((window, b), cols1.dtype),
                pltpu.VMEM((window, b), cols0.dtype),
                pltpu.SemaphoreType.DMA((n_col + 4,)),
            ],
        )
        t_other, t_own = list(out[:nt]), list(out[nt:])
        t_recv = [swap("col", t, 0) for t in t_other]

        def columns(sides, block):
            return kernel(
                functools.partial(column_body, sides, block[0]),
                s,
                [adj, rows1, rows0],
                [f32(block[1], 2 * b)] * len(sides),
                len(sides) * 4 * rows * block[1] * b,
            )

        sums, places = [], []
        for k, block in enumerate(blocks):
            if k == 0:
                (c_other,), (c_own,) = columns((0,), block), columns((1,), block)
            else:
                c_other, c_own = columns((0, 1), block)
            c_recv = swap("row", c_other, 0)
            start, half, cuts = block
            for at in range(0, half, half // cuts):
                cut = slice(at, at + half // cuts)
                sums.append(add(c_own[cut], c_recv[cut]))
                places.append((start + at, half))

        held, theirs = [], []
        for total in sums:
            for bit in range(1, row_bits):
                total = add(total, swap("row", total, bit))
            held.append(total)
            theirs.append(swap("row", total, 0))
        outs = []
        for ks in (range(len(sums) // 2), range(len(sums) // 2, len(sums))):
            args = [held[k] for k in ks] + [theirs[k] for k in ks]
            n = len(args)
            outs = list(
                kernel(
                    functools.partial(write_body, [places[k] for k in ks]),
                    s,
                    args + outs,
                    [f32(window, b)] * 2,
                    specs=[VMEM] * n + [ANY] * len(outs),
                    out_specs=[ANY, ANY],
                    scratch_shapes=[pltpu.SemaphoreType.DMA((2 * n,))],
                    input_output_aliases={n + 1: 0, n + 2: 1} if outs else {},
                )
            )
        col_adj1, col_adj0 = outs

        parts = [("col", k) for k in (1, 0) if k < col_bits]
        swaps = [("col", k) for k in range(2, col_bits)] + [("row", k) for k in range(1, row_bits)]
        pieces = 2 << len(parts)
        data = (b + 1) * (b // LANES)
        total_rows = -(-data // (8 * pieces)) * 8 * pieces
        n1 = sum(p for p, _, _ in shares)
        keep, send = kernel(
            functools.partial(diag_body, blk, n1),
            s,
            [rows1, rows0, p1, p0, inv1, inv0, cross] + t_other + t_own,
            [f32(total_rows // 2, LANES)] * 2,
            15 * rows * b * b + 15 * b**3,
            scratch_shapes=[pltpu.VMEM((b, b), F32)] * 3
            + [pltpu.VMEM((total_rows, LANES), F32)],
        )
        got = swap("row", send, 0)
        for key in parts:
            keep, send = add_split(keep, got, key, keep.shape[0] // 2)
            got = swap(key[0], send, key[1])
        m = add(keep, got)
        for key in swaps:
            m = add(m, swap(key[0], m, key[1]))
        for key in parts:
            m = ordered(key, m, swap(key[0], m, key[1]))
        if len(parts) == 2:
            m = m.reshape(2, 2, -1, LANES).swapaxes(0, 1).reshape(-1, LANES)
        other = swap("row", m, 0)
        d1, d0 = kernel(
            unpack_body,
            s,
            [m, other],
            [f32(b, b)] * 2,
            scratch_shapes=[pltpu.VMEM((total_rows, LANES), F32)],
        )

        trail = {1: [], 0: []}
        for k, share in enumerate(shares):
            keep, got = t_own[k], t_recv[k]
            for bit in range(1, col_bits):
                keep, send = add_split(keep, got, ("col", bit), blk)
                got = swap("col", send, bit)
            trail[share[0]] += [keep, got]
        row1, q = kernel(
            row1_body, s, [p1, p0, inv1, cross] + trail[1], [f32(blk, b)] * 2, 12 * blk * b * b
        )
        (row0,) = kernel(row0_body, s, [q, inv0] + trail[0], [f32(blk, b)], 6 * blk * b * b)
        return row1, row0, col_adj1, col_adj0, d1, d0

    return body


def solution(mesh):
    return jax.shard_map(
        make_local(mesh.shape["row"], mesh.shape["col"]),
        mesh=mesh,
        in_specs=(
            P("row", "col"),
            P("row", None),
            P("row", None),
            P("col", None),
            P("col", None),
            P(),
            P(),
            P(),
            P(("row", "col"), None),
            P(("row", "col"), None),
        ),
        out_specs=(
            P(("row", "col"), None),
            P(("row", "col"), None),
            P("col", None),
            P("col", None),
            P(),
            P(),
        ),
        check_vma=False,
    )
```
